32 devices in a mesh: cand: 8 (over z, x), obs: 4 (over y, core).
Axes of the slice: x: 2, y: 2, z: 4, core: 2. Of those that a mesh axis runs over, the one named last changes fastest.
Arguments:
- block_index: int32 [1], replicated, may hold values from 64 to 127
- slot_block: int32 [128], replicated, may hold values from 0 to 127, each once
- factor_row: bfloat16 [128, 256, 256], P('cand', None, 'obs'), may hold values from -0.03125 to 0.03125
- earlier_rows: bfloat16 [128, 256, 2048], P(None, 'obs', 'cand'), may hold values from -6 to 6
- obs_weights: float32 [128, 256, 32], P('cand'), may hold values from 0.05 to 20
- cand_weights: float32 [2048, 32], P('cand'), may hold values from 0.05 to 20
- block_inverse: float32 [128, 256, 256], P('cand', 'obs'), may hold values from -0.046875 to 0.046875
- prior_var: float32 [2048], P('cand'), may hold values from 16 to 24
Outputs:
- solved_rows: float32 [256, 2048], P('obs', 'cand')
- remaining_var: float32 [2048], P('cand')
The draws below stay inside these ranges and needn't reach their ends.
Inputs may be any that keep to these rules, and one draw needn't show every extreme that they name: slot_block names every block number once.
All inputs are finite; a program needn't handle non-finite values.
Results may differ from the reference program's by a relative error of at most 0.0003.
Values may be sent and summed in bfloat16 or wider, within the bound.
No kernel may reach another device: no remote copies, remote signals or barrier semaphores. Data moves between devices by JAX's collectives and lax.ppermute only.
A program may use at most 64 MiB of HBM per device.

```python
import math
import jax
import jax.numpy as jnp
from jax import lax

DIM = 32
BLK = 256
ORDER = 32768
NBLK = 128
CANDS = 2048


def block_scale(key, extent, split, smallest, high):
    factor_of, own = 1.0, jax.random.fold_in(key, 6)
    for position, shards_of in split:
        draws = jnp.exp(jax.random.uniform(jax.random.fold_in(own, position), (shards_of,), jnp.float32, smallest / len(split), high / len(split)))
        factor_of = factor_of * jnp.repeat(draws, extent[position] // shards_of).reshape([-1 if axis == position else 1 for axis in range(len(extent))])
    return factor_of


def centred(own_key, shape, scale, bound, shards=(), kind=jnp.bfloat16):
    level = block_scale(own_key, shape, shards, -0.22, 0.18) if shards else 1.0
    entries = jax.random.normal(own_key, shape, jnp.float32) * scale * level
    return jnp.minimum(jnp.maximum(entries, -bound), bound).astype(kind)


def setup_inputs(seed: int = 0) -> dict:
    keys = jax.random.split(jax.random.key(seed), 9)
    return {
        "block_index": jax.random.randint(keys[0], (1,), NBLK // 2, NBLK).astype(jnp.int32),
        "slot_block": jax.random.permutation(keys[1], NBLK).astype(jnp.int32),
        "factor_row": centred(keys[2], (NBLK, BLK, BLK), ORDER ** -0.5, 0.03125, ((0, 8), (2, 4))),
        "earlier_rows": centred(keys[3], (NBLK, BLK, CANDS), 1.0, 6.0, ((1, 4), (2, 8))),
        "obs_weights": jnp.clip(jnp.exp(math.log(20.0) - 5.9914645 * jax.random.uniform(keys[4], (NBLK, BLK, DIM), jnp.float32) ** block_scale(keys[4], (NBLK, BLK, DIM), ((0, 8),), -0.2, 0.2)), 0.05, 20.0),
        "cand_weights": jnp.clip(jnp.exp(math.log(20.0) - 5.9914645 * jax.random.uniform(keys[5], (CANDS, DIM), jnp.float32) ** block_scale(keys[5], (CANDS, DIM), ((0, 8),), -0.2, 0.2)), 0.05, 20.0),
        "block_inverse": centred(keys[6], (NBLK, BLK, BLK), (64 * BLK) ** -0.5, 0.046875, ((0, 8), (1, 4)), jnp.float32),
        "prior_var": jnp.clip(16.0 + 8.0 * jax.random.uniform(keys[7], (CANDS,), jnp.float32) ** block_scale(keys[7], (CANDS,), ((0, 8),), -0.2, 0.2), 16.0, 24.0),
    }


HIGH = lax.Precision.HIGHEST


def mixtures(weights):
    return weights / jnp.sum(weights, axis=-1, keepdims=True)


def kernel_tile(points, cands):
    squared = jnp.sum(points * points, axis=-1)[:, None] + jnp.sum(cands * cands, axis=-1)[None, :]
    squared = squared - 2.0 * jnp.dot(points, cands.T, precision=HIGH)
    return jnp.exp(-10.0 * squared)


def reference(block_index, slot_block, factor_row, earlier_rows, obs_weights, cand_weights, block_inverse, prior_var):
    current = block_index[0]
    block_points = mixtures(lax.dynamic_index_in_dim(obs_weights, current, 0, keepdims=False))
    kernel_rows = kernel_tile(block_points, mixtures(cand_weights))

    def add_slot(running, slot):
        block_id = slot_block[slot]
        kept_mask = jnp.where(block_id < current, 1.0, 0.0).astype(jnp.float32)
        earlier = lax.dynamic_index_in_dim(earlier_rows, block_id, 0, keepdims=False).astype(jnp.float32)
        panel_piece = lax.dynamic_index_in_dim(factor_row, slot, 0, keepdims=False).astype(jnp.float32)
        return running + kept_mask * jnp.dot(panel_piece, earlier, precision=HIGH), None

    start_sum = jnp.zeros((factor_row.shape[1], earlier_rows.shape[2]), jnp.float32)
    carried, _ = lax.scan(add_slot, start_sum, jnp.arange(factor_row.shape[0], dtype=jnp.int32))
    inverse = lax.dynamic_index_in_dim(block_inverse, current, 0, keepdims=False)
    solved_rows = jnp.dot(inverse, kernel_rows - carried, precision=HIGH)
    remaining_var = prior_var - jnp.sum(solved_rows * solved_rows, axis=0)
    return (solved_rows, remaining_var)
```

```python
import functools

import jax
import jax.numpy as jnp
from jax import lax
from jax.experimental import pallas as pl
from jax.experimental.pallas import tpu as pltpu
from jax.sharding import PartitionSpec as P

HIGH = lax.Precision.HIGHEST
ROWS = (((0,), (0,)), ((), ()))
VMEM = pl.BlockSpec(memory_space=pltpu.VMEM)
SMEM = pl.BlockSpec(memory_space=pltpu.SMEM)
ANY = pl.BlockSpec(memory_space=pl.ANY)


RING = [(0, 2), (2, 4), (4, 6), (6, 7), (7, 5), (5, 3), (3, 1), (1, 0)]
BACK = [(b, a) for a, b in RING]
OFFSETS = (-1, 1, -2, 2, -3, 3, 0, 4)
LIMIT = 16 * 2**20


def ring_holder(place):
    place = lax.rem(place + 8, 8)
    return jnp.where(place < 4, 2 * place, 2 * (7 - place) + 1)


def panel_product(panel, rows):
    left = panel.reshape(rows.shape[0], panel.shape[-1])
    return lax.dot_general(left, rows, ROWS, preferred_element_type=jnp.float32)


def collect_kernel(slot_block, current, panel, earlier, rows, total, sem):
    slots, depth = panel.shape[:2]
    cand = lax.axis_index("cand")
    place = jnp.where(lax.rem(cand, 2) == 0, cand // 2, 7 - cand // 2)
    for i, offset in enumerate(OFFSETS):
        base = ring_holder(place + offset) * slots

        @pl.loop(0, slots)
        def _(s):
            block = slot_block[base + s]
            pltpu.make_async_copy(earlier.at[block], rows.at[i * slots + s], sem).start()

    pltpu.make_async_copy(earlier, rows, sem).wait()
    for i, offset in enumerate(OFFSETS):
        base = ring_holder(place + offset) * slots

        @pl.loop(0, slots)
        def _(s):
            @pl.when(slot_block[base + s] >= current[0])
            def _():
                rows[i * slots + s] = jnp.zeros(rows.shape[1:], rows.dtype)

    own = OFFSETS.index(0) * slots
    total[...] = panel_product(panel[...], rows[own : own + slots].reshape(slots * depth, rows.shape[-1]))


def collect(slot_block, current, panel, earlier):
    rows, cols = panel.shape[2], earlier.shape[-1]
    return pl.pallas_call(
        collect_kernel,
        out_shape=[
            jax.ShapeDtypeStruct(earlier.shape, earlier.dtype),
            jax.ShapeDtypeStruct((rows, cols), jnp.float32),
        ],
        in_specs=[SMEM, SMEM, VMEM, ANY],
        out_specs=[VMEM, VMEM],
        scratch_shapes=[pltpu.SemaphoreType.DMA],
        compiler_params=pltpu.CompilerParams(vmem_limit_bytes=LIMIT),
        cost_estimate=pl.CostEstimate(
            flops=2 * panel.size * cols, bytes_accessed=4 * earlier.size, transcendentals=0
        ),
    )(slot_block, current, panel, earlier)


def add_kernel(panel_a, panel_b, rows, before, total):
    half = rows.shape[0] * rows.shape[1] // 2
    right = rows[...].reshape(2 * half, rows.shape[-1])
    value = panel_product(panel_a[...], right[:half]) + panel_product(panel_b[...], right[half:])
    total[...] = before[...] + value


def add_last_kernel(panel_a, panel_b, rows, before, mine, other):
    half = rows.shape[0] * rows.shape[1] // 2
    right = rows[...].reshape(2 * half, rows.shape[-1])
    value = panel_product(panel_a[...], right[:half]) + panel_product(panel_b[...], right[half:])
    value = before[...] + value
    size = mine.shape[0]
    first = lax.rem(lax.axis_index("obs"), 2) == 0
    mine[...] = jnp.where(first, value[:size], value[size:])
    other[...] = jnp.where(first, value[size:], value[:size])


def add(panels, rows, position, before, last=False):
    slots, depth, size = panels[0].shape
    cols = rows.shape[-1]
    shape = (size // 2, cols) if last else (size, cols)
    return pl.pallas_call(
        add_last_kernel if last else add_kernel,
        grid=(1,),
        out_shape=[jax.ShapeDtypeStruct(shape, jnp.float32)] * (2 if last else 1),
        in_specs=[
            pl.BlockSpec(panels[0].shape, lambda i: (0, 0, 0)),
            pl.BlockSpec(panels[0].shape, lambda i: (0, 0, 0)),
            pl.BlockSpec((2 * slots, depth, cols), lambda i: (position, 0, 0)),
            pl.BlockSpec((size, cols), lambda i: (0, 0)),
        ],
        out_specs=[pl.BlockSpec(shape, lambda i: (0, 0))] * (2 if last else 1),
        compiler_params=pltpu.CompilerParams(vmem_limit_bytes=LIMIT),
        cost_estimate=pl.CostEstimate(
            flops=4 * panels[0].size * cols, bytes_accessed=8 * panels[0].size, transcendentals=0
        ),
    )(*panels, rows, before)


def tile_kernel(spread_0, spread_1, spread_2, spread_3, cands, tile, points):
    obs = lax.axis_index("obs")
    share = points.shape[0] // 4
    for m, spread in enumerate((spread_0, spread_1, spread_2, spread_3)):
        points[pl.ds(pl.multiple_of((obs ^ m) * share, share), share), :] = spread[-share:, :]
    p = points[...]
    p = p / jnp.sum(p, axis=0, keepdims=True)
    c = cands[...]
    c = c / jnp.sum(c, axis=0, keepdims=True)
    cross = lax.dot_general(p, c, ROWS, precision=HIGH, preferred_element_type=jnp.float32)
    norms = lax.dot_general(p * p, jnp.ones_like(c), ROWS, precision=HIGH, preferred_element_type=jnp.float32)
    squared = norms + jnp.sum(c * c, axis=0, keepdims=True) - 2.0 * cross
    tile[...] = jnp.exp(-10.0 * squared)


def solve_kernel(mine, other, mate, far, mate_far, tile, s0, s1, s2, s3, prior, solved, remaining, residual):
    half, rows = mine.shape[0], solved.shape[0]
    core = lax.rem(lax.axis_index("obs"), 2)
    first = pl.ds(pl.multiple_of(core * half, half), half)
    second = pl.ds(pl.multiple_of((1 - core) * half, half), half)
    residual[first, :] = tile[first, :] - (mine[...] + mate[half:, :] + far[...])
    residual[second, :] = tile[second, :] - (other[...] + mate[:half, :] + mate_far[...])
    value = residual[...]
    squares = jnp.zeros(remaining.shape, jnp.float32)
    for m, spread in enumerate((s0, s1, s2, s3)):
        part = jnp.dot(spread[:rows, :], value, precision=HIGH, preferred_element_type=jnp.float32)
        squares += jnp.sum(part * part, axis=0, keepdims=True)
        if m == 0:
            solved[...] = part
    remaining[...] = prior[...] - squares


def on_ring(
    block_index,
    slot_block,
    factor_row,
    earlier_rows,
    obs_weights,
    cand_weights,
    block_inverse,
    prior_var,
):
    cand, obs = lax.axis_index("cand"), lax.axis_index("obs")
    current = block_index[0]
    held = obs_weights.shape[0]
    half = held // 2
    cols = earlier_rows.shape[2]
    panel = jnp.swapaxes(factor_row, 1, 2)

    def flip(value, axis, bits, size):
        return lax.ppermute(value, axis, [(i, i ^ bits) for i in range(size)])

    slot_here = current % held
    inverse_rows = lax.dynamic_index_in_dim(block_inverse, slot_here, 0, keepdims=False)
    points = lax.dynamic_index_in_dim(jnp.swapaxes(obs_weights, 1, 2), slot_here, 0, keepdims=False)
    share = points.shape[0] // 4
    points = lax.dynamic_slice_in_dim(points, obs * share, share, 0)
    spread = jnp.concatenate([inverse_rows, points], axis=0)
    spread = jnp.where(cand == current // held, spread, jnp.zeros_like(spread))

    tie = lax.optimization_barrier
    forward = [panel, lax.ppermute(panel, "cand", RING)]
    backward = [panel, lax.ppermute(panel, "cand", BACK)]
    rows, total = collect(slot_block, block_index, panel, earlier_rows)
    spread = spread + flip(spread, "cand", 1, 8)
    forward[1], backward[1], rows, total, spread = tie((forward[1], backward[1], rows, total, spread))

    forward.append(lax.ppermute(forward[1], "cand", RING))
    backward.append(lax.ppermute(backward[1], "cand", BACK))
    (total,) = add([forward[1], backward[1]], rows, 0, total)
    spread = spread + flip(spread, "cand", 2, 8)
    spread = spread + flip(spread, "cand", 4, 8)
    forward[2], backward[2], total, spread = tie((forward[2], backward[2], total, spread))

    forward.append(lax.ppermute(forward[2], "cand", RING))
    backward.append(lax.ppermute(backward[2], "cand", BACK))
    (total,) = add([forward[2], backward[2]], rows, 1, total)
    spreads = [spread, flip(spread, "obs", 1, 4)]
    spreads += [flip(spreads[0], "obs", 2, 4), flip(spreads[1], "obs", 2, 4)]
    forward[3], backward[3], total, spreads = tie((forward[3], backward[3], total, spreads))

    forward.append(lax.ppermute(forward[3][:half], "cand", RING))
    backward.append(lax.ppermute(backward[3][half:], "cand", BACK))
    (total,) = add([forward[3], backward[3]], rows, 2, total)
    tile = pl.pallas_call(
        tile_kernel,
        out_shape=jax.ShapeDtypeStruct((panel.shape[2], cols), jnp.float32),
        in_specs=[VMEM] * 5,
        out_specs=VMEM,
        scratch_shapes=[pltpu.VMEM((obs_weights.shape[2], panel.shape[2]), jnp.float32)],
        compiler_params=pltpu.CompilerParams(vmem_limit_bytes=LIMIT),
        cost_estimate=pl.CostEstimate(flops=10**7, bytes_accessed=10**6, transcendentals=65536),
    )(*spreads, cand_weights.T)

    forward[4], backward[4], total, tile = tie((forward[4], backward[4], total, tile))
    mine, other = add([forward[4], backward[4]], rows, OFFSETS.index(4), total, last=True)

    mate = flip(jnp.concatenate([mine, other], axis=0), "obs", 1, 4)
    far = flip(mine + mate[mine.shape[0] :], "obs", 2, 4)
    mate_far = flip(far, "obs", 1, 4)
    solved_rows, remaining = pl.pallas_call(
        solve_kernel,
        out_shape=[
            jax.ShapeDtypeStruct(inverse_rows.shape[:1] + (cols,), jnp.float32),
            jax.ShapeDtypeStruct((1, cols), jnp.float32),
        ],
        in_specs=[VMEM] * 11,
        out_specs=[VMEM] * 2,
        scratch_shapes=[pltpu.VMEM((panel.shape[2], cols), jnp.float32)],
        compiler_params=pltpu.CompilerParams(vmem_limit_bytes=LIMIT),
        cost_estimate=pl.CostEstimate(flops=2 * 10**8, bytes_accessed=10**6, transcendentals=0),
    )(mine, other, mate, far, mate_far, tile, *spreads, prior_var[None])
    return (solved_rows, remaining[0])


def kernel_tile(points, cands):
    points = points / jnp.sum(points, axis=0, keepdims=True)
    cands = cands / jnp.sum(cands, axis=0, keepdims=True)
    squared = jnp.sum(points * points, axis=0)[:, None] + jnp.sum(cands * cands, axis=0)[None, :]
    squared = squared - 2.0 * lax.dot_general(points, cands, ROWS, precision=HIGH)
    return jnp.exp(-10.0 * squared)


def spread_all(block, axis, holder):
    block = jnp.where(lax.axis_index(axis) == holder, block, jnp.zeros_like(block))
    return lax.psum(block, axis)


def on_any(
    block_index,
    slot_block,
    factor_row,
    earlier_rows,
    obs_weights,
    cand_weights,
    block_inverse,
    prior_var,
):
    current = block_index[0]
    held = obs_weights.shape[0]
    points = lax.dynamic_index_in_dim(obs_weights, current % held, 0, keepdims=False)
    inverse_rows = lax.dynamic_index_in_dim(block_inverse, current % held, 0, keepdims=False)
    points = spread_all(points, "cand", current // held)
    inverse_rows = spread_all(inverse_rows, "cand", current // held)
    kernel_rows = kernel_tile(points.T, cand_weights.T)
    panel = lax.all_gather(factor_row, "cand", axis=0, tiled=True)
    panel = panel * (slot_block < current).astype(jnp.bfloat16)[:, None, None]
    earlier = jnp.take(earlier_rows, slot_block, axis=0)
    partial_sum = jnp.einsum("stq,sqc->tc", panel, earlier, preferred_element_type=jnp.float32)
    residual = kernel_rows - lax.psum(partial_sum, "obs")
    solved_rows = jnp.dot(inverse_rows, residual, precision=HIGH)
    square_sums = lax.psum(jnp.sum(solved_rows * solved_rows, axis=0), "obs")
    return (solved_rows, prior_var - square_sums)


def solution(mesh):
    placed = (
        P(),
        P(),
        P("cand", None, "obs"),
        P(None, "obs", "cand"),
        P("cand", None, None),
        P("cand", None),
        P("cand", "obs", None),
        P("cand"),
    )
    small = mesh.shape["cand"] == 8 and mesh.shape["obs"] == 4
    return jax.shard_map(
        on_ring if small else on_any,
        mesh=mesh,
        in_specs=placed,
        out_specs=(P("obs", "cand"), P("cand")),
        check_vma=False,
    )
```

```python
import functools

import jax
import jax.numpy as jnp
from jax import lax
from jax.experimental import pallas as pl
from jax.experimental.pallas import tpu as pltpu
from jax.sharding import PartitionSpec as P

HIGH = lax.Precision.HIGHEST
ROWS = (((0,), (0,)), ((), ()))
VMEM = pl.BlockSpec(memory_space=pltpu.VMEM)
SMEM = pl.BlockSpec(memory_space=pltpu.SMEM)
ANY = pl.BlockSpec(memory_space=pl.ANY)


RING = [(0, 2), (2, 4), (4, 6), (6, 7), (7, 5), (5, 3), (3, 1), (1, 0)]
BACK = [(b, a) for a, b in RING]
LIMIT = 16 * 2**20


def ring_holder(place):
    place = lax.rem(place + 8, 8)
    return jnp.where(place < 4, 2 * place, 2 * (7 - place) + 1)


def partial_sum(sources, slot_block, current, panels, earlier, rows):
    cand = lax.axis_index("cand")
    place = jnp.where(lax.rem(cand, 2) == 0, cand // 2, 7 - cand // 2)
    slots, depth, _ = panels[0].shape
    value = None
    for j, (offset, first, held) in enumerate(sources):
        base = ring_holder(place + offset) * held + first
        for s in range(slots):
            block = slot_block[base + s]
            kept = (block < current[0]).astype(jnp.float32).astype(rows.dtype)
            rows[j, s * depth : (s + 1) * depth, :] = earlier[block] * kept
        left = panels[j][...].reshape(slots * depth, panels[j].shape[-1])
        term = lax.dot_general(left, rows[j], ROWS, preferred_element_type=jnp.float32)
        value = term if value is None else value + term
    return value


def own_kernel(sources, slot_block, current, panel, earlier, total, rows):
    total[...] = partial_sum(sources, slot_block, current, [panel], earlier, rows)


def add_kernel(sources, slot_block, current, *refs):
    *panels, earlier, before, total, rows = refs
    total[...] = before[...] + partial_sum(sources, slot_block, current, panels, earlier, rows)


def last_kernel(sources, slot_block, current, panel_a, panel_b, earlier, before, mine, other, rows):
    value = before[...] + partial_sum(sources, slot_block, current, [panel_a, panel_b], earlier, rows)
    size = mine.shape[0]
    first = lax.rem(lax.axis_index("obs"), 2) == 0
    mine[...] = jnp.where(first, value[:size], value[size:])
    other[...] = jnp.where(first, value[size:], value[:size])


def add(kernel, sources, slot_block, current, panels, earlier, before=()):
    slots, depth, size = panels[0].shape
    cols = earlier.shape[-1]
    shapes = [(size // 2, cols)] * 2 if kernel is last_kernel else [(size, cols)]
    return pl.pallas_call(
        functools.partial(kernel, sources),
        out_shape=[jax.ShapeDtypeStruct(shape, jnp.float32) for shape in shapes],
        in_specs=[SMEM] * 2 + [VMEM] * (len(panels) + 1 + len(before)),
        out_specs=[VMEM] * len(shapes),
        scratch_shapes=[pltpu.VMEM((len(panels), slots * depth, cols), earlier.dtype)],
        compiler_params=pltpu.CompilerParams(vmem_limit_bytes=LIMIT),
        cost_estimate=pl.CostEstimate(
            flops=2 * len(panels) * panels[0].size * cols,
            bytes_accessed=4 * len(panels) * panels[0].size,
            transcendentals=0,
        ),
    )(slot_block, current, *panels, earlier, *before)


def tile_kernel(spread_0, spread_1, spread_2, spread_3, cands, tile, points):
    obs = lax.axis_index("obs")
    share = points.shape[0] // 4
    for m, spread in enumerate((spread_0, spread_1, spread_2, spread_3)):
        points[pl.ds(pl.multiple_of((obs ^ m) * share, share), share), :] = spread[-share:, :]
    p = points[...]
    p = p / jnp.sum(p, axis=0, keepdims=True)
    c = cands[...]
    c = c / jnp.sum(c, axis=0, keepdims=True)
    cross = lax.dot_general(p, c, ROWS, precision=HIGH, preferred_element_type=jnp.float32)
    norms = lax.dot_general(p * p, jnp.ones_like(c), ROWS, precision=HIGH, preferred_element_type=jnp.float32)
    squared = norms + jnp.sum(c * c, axis=0, keepdims=True) - 2.0 * cross
    tile[...] = jnp.exp(-10.0 * squared)


def solve_kernel(mine, other, mate, far, mate_far, tile, s0, s1, s2, s3, prior, solved, remaining, residual):
    half, rows = mine.shape[0], solved.shape[0]
    core = lax.rem(lax.axis_index("obs"), 2)
    first = pl.ds(pl.multiple_of(core * half, half), half)
    second = pl.ds(pl.multiple_of((1 - core) * half, half), half)
    residual[first, :] = tile[first, :] - (mine[...] + mate[half:, :] + far[...])
    residual[second, :] = tile[second, :] - (other[...] + mate[:half, :] + mate_far[...])
    value = residual[...]
    squares = jnp.zeros(remaining.shape, jnp.float32)
    for m, spread in enumerate((s0, s1, s2, s3)):
        part = jnp.dot(spread[:rows, :], value, precision=HIGH, preferred_element_type=jnp.float32)
        squares += jnp.sum(part * part, axis=0, keepdims=True)
        if m == 0:
            solved[...] = part
    remaining[...] = prior[...] - squares


def on_ring(
    block_index,
    slot_block,
    factor_row,
    earlier_rows,
    obs_weights,
    cand_weights,
    block_inverse,
    prior_var,
):
    cand, obs = lax.axis_index("cand"), lax.axis_index("obs")
    current = block_index[0]
    held = obs_weights.shape[0]
    half = held // 2
    cols = earlier_rows.shape[2]
    panel = jnp.swapaxes(factor_row, 1, 2)

    def flip(value, axis, bits, size):
        return lax.ppermute(value, axis, [(i, i ^ bits) for i in range(size)])

    slot_here = current % held
    inverse_rows = lax.dynamic_index_in_dim(block_inverse, slot_here, 0, keepdims=False)
    points = lax.dynamic_index_in_dim(jnp.swapaxes(obs_weights, 1, 2), slot_here, 0, keepdims=False)
    share = points.shape[0] // 4
    points = lax.dynamic_slice_in_dim(points, obs * share, share, 0)
    spread = jnp.concatenate([inverse_rows, points], axis=0)
    spread = jnp.where(cand == current // held, spread, jnp.zeros_like(spread))

    tie = lax.optimization_barrier

    def onward(pair):
        return (lax.ppermute(pair[0], "cand", RING), lax.ppermute(pair[1], "cand", BACK))

    early = onward((panel[:half], panel[:half]))
    late = onward((panel[half:], panel[half:]))
    (total,) = add(own_kernel, [(0, 0, held)], slot_block, block_index, [panel], earlier_rows)
    spread = spread + flip(spread, "cand", 1, 8)
    for k in (1, 2, 3):
        next_early = onward(early) if k < 3 else lax.ppermute(early[0], "cand", RING)
        late, total, spread = tie((late, total, spread))
        next_late = onward(late) if k < 3 else lax.ppermute(late[1], "cand", BACK)
        sources = [(-k, 0, held), (k, 0, held), (-k, half, held), (k, half, held)]
        (total,) = add(add_kernel, sources, slot_block, block_index, [*early, *late], earlier_rows, [total])
        if k < 3:
            spread = spread + flip(spread, "cand", 2 * k, 8)
        early, late = next_early, next_late
    spreads = [spread, flip(spread, "obs", 1, 4)]
    spreads += [flip(spreads[0], "obs", 2, 4), flip(spreads[1], "obs", 2, 4)]
    tile = pl.pallas_call(
        tile_kernel,
        out_shape=jax.ShapeDtypeStruct((panel.shape[2], cols), jnp.float32),
        in_specs=[VMEM] * 5,
        out_specs=VMEM,
        scratch_shapes=[pltpu.VMEM((obs_weights.shape[2], panel.shape[2]), jnp.float32)],
        compiler_params=pltpu.CompilerParams(vmem_limit_bytes=LIMIT),
        cost_estimate=pl.CostEstimate(flops=10**7, bytes_accessed=10**6, transcendentals=65536),
    )(*spreads, cand_weights.T)

    early, late, total, tile = tie((early, late, total, tile))
    sources = [(-4, 0, held), (4, half, held)]
    mine, other = add(last_kernel, sources, slot_block, block_index, [early, late], earlier_rows, [total])

    mate = flip(jnp.concatenate([mine, other], axis=0), "obs", 1, 4)
    far = flip(mine + mate[mine.shape[0] :], "obs", 2, 4)
    mate_far = flip(far, "obs", 1, 4)
    solved_rows, remaining = pl.pallas_call(
        solve_kernel,
        out_shape=[
            jax.ShapeDtypeStruct(inverse_rows.shape[:1] + (cols,), jnp.float32),
            jax.ShapeDtypeStruct((1, cols), jnp.float32),
        ],
        in_specs=[VMEM] * 11,
        out_specs=[VMEM] * 2,
        scratch_shapes=[pltpu.VMEM((panel.shape[2], cols), jnp.float32)],
        compiler_params=pltpu.CompilerParams(vmem_limit_bytes=LIMIT),
        cost_estimate=pl.CostEstimate(flops=2 * 10**8, bytes_accessed=10**6, transcendentals=0),
    )(mine, other, mate, far, mate_far, tile, *spreads, prior_var[None])
    return (solved_rows, remaining[0])


def kernel_tile(points, cands):
    points = points / jnp.sum(points, axis=0, keepdims=True)
    cands = cands / jnp.sum(cands, axis=0, keepdims=True)
    squared = jnp.sum(points * points, axis=0)[:, None] + jnp.sum(cands * cands, axis=0)[None, :]
    squared = squared - 2.0 * lax.dot_general(points, cands, ROWS, precision=HIGH)
    return jnp.exp(-10.0 * squared)


def spread_all(block, axis, holder):
    block = jnp.where(lax.axis_index(axis) == holder, block, jnp.zeros_like(block))
    return lax.psum(block, axis)


def on_any(
    block_index,
    slot_block,
    factor_row,
    earlier_rows,
    obs_weights,
    cand_weights,
    block_inverse,
    prior_var,
):
    current = block_index[0]
    held = obs_weights.shape[0]
    points = lax.dynamic_index_in_dim(obs_weights, current % held, 0, keepdims=False)
    inverse_rows = lax.dynamic_index_in_dim(block_inverse, current % held, 0, keepdims=False)
    points = spread_all(points, "cand", current // held)
    inverse_rows = spread_all(inverse_rows, "cand", current // held)
    kernel_rows = kernel_tile(points.T, cand_weights.T)
    panel = lax.all_gather(factor_row, "cand", axis=0, tiled=True)
    panel = panel * (slot_block < current).astype(jnp.bfloat16)[:, None, None]
    earlier = jnp.take(earlier_rows, slot_block, axis=0)
    partial_sum = jnp.einsum("stq,sqc->tc", panel, earlier, preferred_element_type=jnp.float32)
    residual = kernel_rows - lax.psum(partial_sum, "obs")
    solved_rows = jnp.dot(inverse_rows, residual, precision=HIGH)
    square_sums = lax.psum(jnp.sum(solved_rows * solved_rows, axis=0), "obs")
    return (solved_rows, prior_var - square_sums)


def solution(mesh):
    placed = (
        P(),
        P(),
        P("cand", None, "obs"),
        P(None, "obs", "cand"),
        P("cand", None, None),
        P("cand", None),
        P("cand", "obs", None),
        P("cand"),
    )
    small = mesh.shape["cand"] == 8 and mesh.shape["obs"] == 4
    return jax.shard_map(
        on_ring if small else on_any,
        mesh=mesh,
        in_specs=placed,
        out_specs=(P("obs", "cand"), P("cand")),
        check_vma=False,
    )
```

```python
import functools

import jax
import jax.numpy as jnp
from jax import lax
from jax.experimental import pallas as pl
from jax.experimental.pallas import tpu as pltpu
from jax.sharding import PartitionSpec as P

HIGH = lax.Precision.HIGHEST
ROWS = (((0,), (0,)), ((), ()))
VMEM = pl.BlockSpec(memory_space=pltpu.VMEM)
SMEM = pl.BlockSpec(memory_space=pltpu.SMEM)
ANY = pl.BlockSpec(memory_space=pl.ANY)


RING = [(0, 2), (2, 4), (4, 6), (6, 7), (7, 5), (5, 3), (3, 1), (1, 0)]
BACK = [(b, a) for a, b in RING]
LIMIT = 16 * 2**20


def ring_holder(place):
    place = lax.rem(place + 8, 8)
    return jnp.where(place < 4, 2 * place, 2 * (7 - place) + 1)


def partial_sum(sources, slot_block, current, panels, earlier, rows):
    cand = lax.axis_index("cand")
    place = jnp.where(lax.rem(cand, 2) == 0, cand // 2, 7 - cand // 2)
    slots, depth, _ = panels[0].shape
    value = None
    for j, (offset, first, held) in enumerate(sources):
        base = ring_holder(place + offset) * held + first
        for s in range(slots):
            block = slot_block[base + s]
            kept = (block < current[0]).astype(jnp.float32).astype(rows.dtype)
            rows[j, s * depth : (s + 1) * depth, :] = earlier[block] * kept
        left = panels[j][...].reshape(slots * depth, panels[j].shape[-1])
        term = lax.dot_general(left, rows[j], ROWS, preferred_element_type=jnp.float32)
        value = term if value is None else value + term
    return value


def own_kernel(sources, slot_block, current, panel, earlier, total, rows):
    total[...] = partial_sum(sources, slot_block, current, [panel], earlier, rows)


def add_kernel(sources, slot_block, current, *refs):
    *panels, earlier, before, total, rows = refs
    total[...] = before[...] + partial_sum(sources, slot_block, current, panels, earlier, rows)


def last_kernel(sources, slot_block, current, panel_a, panel_b, earlier, before, mine, other, rows):
    value = before[...] + partial_sum(sources, slot_block, current, [panel_a, panel_b], earlier, rows)
    size = mine.shape[0]
    first = lax.rem(lax.axis_index("obs"), 2) == 0
    mine[...] = jnp.where(first, value[:size], value[size:])
    other[...] = jnp.where(first, value[size:], value[:size])


def add(kernel, sources, slot_block, current, panels, earlier, before=()):
    slots, depth, size = panels[0].shape
    cols = earlier.shape[-1]
    shapes = [(size // 2, cols)] * 2 if kernel is last_kernel else [(size, cols)]
    return pl.pallas_call(
        functools.partial(kernel, sources),
        out_shape=[jax.ShapeDtypeStruct(shape, jnp.float32) for shape in shapes],
        in_specs=[SMEM] * 2 + [VMEM] * (len(panels) + 1 + len(before)),
        out_specs=[VMEM] * len(shapes),
        scratch_shapes=[pltpu.VMEM((len(panels), slots * depth, cols), earlier.dtype)],
        compiler_params=pltpu.CompilerParams(vmem_limit_bytes=LIMIT),
        cost_estimate=pl.CostEstimate(
            flops=2 * len(panels) * panels[0].size * cols,
            bytes_accessed=4 * len(panels) * panels[0].size,
            transcendentals=0,
        ),
    )(slot_block, current, *panels, earlier, *before)


def tile_kernel(held, given, cands, tile, high, low, points):
    obs = lax.axis_index("obs")
    side = lax.rem(lax.axis_index("cand"), 2)
    share = points.shape[0] // 4
    size = held.shape[0] // 4
    rows = size - share
    for m in range(4):
        points[pl.ds(pl.multiple_of((obs ^ m) * share, share), share), :] = held[m * size + rows : (m + 1) * size, :]
        for piece, place in ((held, side), (given, 1 - side)):
            inverse = piece[m * size : m * size + rows, :]
            top = inverse.astype(jnp.bfloat16)
            here = pl.ds(pl.multiple_of((2 * m + place) * rows, rows), rows)
            high[here, :] = top
            low[here, :] = (inverse - top.astype(jnp.float32)).astype(jnp.bfloat16)
    p = points[...]
    p = p / jnp.sum(p, axis=0, keepdims=True)
    c = cands[...]
    c = c / jnp.sum(c, axis=0, keepdims=True)
    cross = lax.dot_general(p, c, ROWS, precision=HIGH, preferred_element_type=jnp.float32)
    norms = lax.dot_general(p * p, jnp.ones_like(c), ROWS, precision=HIGH, preferred_element_type=jnp.float32)
    squared = norms + jnp.sum(c * c, axis=0, keepdims=True) - 2.0 * cross
    tile[...] = jnp.exp(-10.0 * squared)


def solve_kernel(mine, other, mate, far, mate_far, tile, high, low, prior, solved, remaining, residual):
    half, rows = mine.shape[0], solved.shape[0]
    core = lax.rem(lax.axis_index("obs"), 2)
    first = pl.ds(pl.multiple_of(core * half, half), half)
    second = pl.ds(pl.multiple_of((1 - core) * half, half), half)
    residual[first, :] = tile[first, :] - (mine[...] + mate[half:, :] + far[...])
    residual[second, :] = tile[second, :] - (other[...] + mate[:half, :] + mate_far[...])
    value = residual[...]
    top = value.astype(jnp.bfloat16)
    rest = (value - top.astype(jnp.float32)).astype(jnp.bfloat16)
    part = jnp.dot(low[...], top, preferred_element_type=jnp.float32)
    part += jnp.dot(high[...], rest, preferred_element_type=jnp.float32)
    part += jnp.dot(high[...], top, preferred_element_type=jnp.float32)
    solved[...] = part[:rows]
    remaining[...] = prior[...] - jnp.sum(part * part, axis=0, keepdims=True)


def on_ring(
    block_index,
    slot_block,
    factor_row,
    earlier_rows,
    obs_weights,
    cand_weights,
    block_inverse,
    prior_var,
):
    cand, obs = lax.axis_index("cand"), lax.axis_index("obs")
    current = block_index[0]
    held = obs_weights.shape[0]
    half = held // 2
    cols = earlier_rows.shape[2]
    panel = jnp.swapaxes(factor_row, 1, 2)

    def flip(value, axis, bits, size):
        return lax.ppermute(value, axis, [(i, i ^ bits) for i in range(size)])

    slot_here = current % held
    points = lax.dynamic_index_in_dim(jnp.swapaxes(obs_weights, 1, 2), slot_here, 0, keepdims=False)
    share = points.shape[0] // 4
    points = lax.dynamic_slice_in_dim(points, obs * share, share, 0)
    rows, width = block_inverse.shape[1:]

    def rows_of(side):
        part = lax.dynamic_slice(block_inverse, (slot_here, side * (rows // 2), 0), (1, rows // 2, width))[0]
        part = jnp.concatenate([part, points], axis=0)
        return jnp.where(cand == current // held, part, jnp.zeros_like(part))

    spread, gift = rows_of(cand % 2), rows_of(1 - cand % 2)

    tie = lax.optimization_barrier

    def onward(pair):
        return (lax.ppermute(pair[0], "cand", RING), lax.ppermute(pair[1], "cand", BACK))

    early = onward((panel[:half], panel[:half]))
    late = onward((panel[half:], panel[half:]))
    (total,) = add(own_kernel, [(0, 0, held)], slot_block, block_index, [panel], earlier_rows)
    spread = spread + flip(gift, "cand", 1, 8)
    for k in (1, 2, 3):
        next_early = onward(early) if k < 3 else lax.ppermute(early[0], "cand", RING)
        late, total, spread = tie((late, total, spread))
        next_late = onward(late) if k < 3 else lax.ppermute(late[1], "cand", BACK)
        sources = [(-k, 0, held), (k, 0, held), (-k, half, held), (k, half, held)]
        (total,) = add(add_kernel, sources, slot_block, block_index, [*early, *late], earlier_rows, [total])
        if k < 3:
            spread = spread + flip(spread, "cand", 2 * k, 8)
        early, late = next_early, next_late
    spreads = [spread, flip(spread, "obs", 1, 4)]
    spreads += [flip(spreads[0], "obs", 2, 4), flip(spreads[1], "obs", 2, 4)]
    early, late, total, spreads = tie((early, late, total, spreads))
    spread = jnp.concatenate(spreads, axis=0)
    given = flip(spread, "cand", 1, 8)
    sources = [(-4, 0, held), (4, half, held)]
    mine, other = add(last_kernel, sources, slot_block, block_index, [early, late], earlier_rows, [total])

    size = panel.shape[2]
    tile, high, low = pl.pallas_call(
        tile_kernel,
        out_shape=[
            jax.ShapeDtypeStruct((size, cols), jnp.float32),
            jax.ShapeDtypeStruct((4 * rows, size), jnp.bfloat16),
            jax.ShapeDtypeStruct((4 * rows, size), jnp.bfloat16),
        ],
        in_specs=[VMEM] * 3,
        out_specs=[VMEM] * 3,
        scratch_shapes=[pltpu.VMEM((obs_weights.shape[2], size), jnp.float32)],
        compiler_params=pltpu.CompilerParams(vmem_limit_bytes=LIMIT),
        cost_estimate=pl.CostEstimate(flops=10**7, bytes_accessed=10**6, transcendentals=65536),
    )(spread, given, cand_weights.T)

    mate = flip(jnp.concatenate([mine, other], axis=0), "obs", 1, 4)
    far = flip(mine + mate[mine.shape[0] :], "obs", 2, 4)
    mate_far = flip(far, "obs", 1, 4)
    solved_rows, remaining = pl.pallas_call(
        solve_kernel,
        out_shape=[
            jax.ShapeDtypeStruct((rows, cols), jnp.float32),
            jax.ShapeDtypeStruct((1, cols), jnp.float32),
        ],
        in_specs=[VMEM] * 9,
        out_specs=[VMEM] * 2,
        scratch_shapes=[pltpu.VMEM((panel.shape[2], cols), jnp.float32)],
        compiler_params=pltpu.CompilerParams(vmem_limit_bytes=LIMIT),
        cost_estimate=pl.CostEstimate(flops=2 * 10**8, bytes_accessed=10**6, transcendentals=0),
    )(mine, other, mate, far, mate_far, tile, high, low, prior_var[None])
    return (solved_rows, remaining[0])


def kernel_tile(points, cands):
    points = points / jnp.sum(points, axis=0, keepdims=True)
    cands = cands / jnp.sum(cands, axis=0, keepdims=True)
    squared = jnp.sum(points * points, axis=0)[:, None] + jnp.sum(cands * cands, axis=0)[None, :]
    squared = squared - 2.0 * lax.dot_general(points, cands, ROWS, precision=HIGH)
    return jnp.exp(-10.0 * squared)


def spread_all(block, axis, holder):
    block = jnp.where(lax.axis_index(axis) == holder, block, jnp.zeros_like(block))
    return lax.psum(block, axis)


def on_any(
    block_index,
    slot_block,
    factor_row,
    earlier_rows,
    obs_weights,
    cand_weights,
    block_inverse,
    prior_var,
):
    current = block_index[0]
    held = obs_weights.shape[0]
    points = lax.dynamic_index_in_dim(obs_weights, current % held, 0, keepdims=False)
    inverse_rows = lax.dynamic_index_in_dim(block_inverse, current % held, 0, keepdims=False)
    points = spread_all(points, "cand", current // held)
    inverse_rows = spread_all(inverse_rows, "cand", current // held)
    kernel_rows = kernel_tile(points.T, cand_weights.T)
    panel = lax.all_gather(factor_row, "cand", axis=0, tiled=True)
    panel = panel * (slot_block < current).astype(jnp.bfloat16)[:, None, None]
    earlier = jnp.take(earlier_rows, slot_block, axis=0)
    partial_sum = jnp.einsum("stq,sqc->tc", panel, earlier, preferred_element_type=jnp.float32)
    residual = kernel_rows - lax.psum(partial_sum, "obs")
    solved_rows = jnp.dot(inverse_rows, residual, precision=HIGH)
    square_sums = lax.psum(jnp.sum(solved_rows * solved_rows, axis=0), "obs")
    return (solved_rows, prior_var - square_sums)


def solution(mesh):
    placed = (
        P(),
        P(),
        P("cand", None, "obs"),
        P(None, "obs", "cand"),
        P("cand", None, None),
        P("cand", None),
        P("cand", "obs", None),
        P("cand"),
    )
    small = mesh.shape["cand"] == 8 and mesh.shape["obs"] == 4
    return jax.shard_map(
        on_ring if small else on_any,
        mesh=mesh,
        in_specs=placed,
        out_specs=(P("obs", "cand"), P("cand")),
        check_vma=False,
    )
```

```python
import functools

import jax
import jax.numpy as jnp
from jax import lax
from jax.experimental import pallas as pl
from jax.experimental.pallas import tpu as pltpu
from jax.sharding import PartitionSpec as P

HIGH = lax.Precision.HIGHEST
ROWS = (((0,), (0,)), ((), ()))
VMEM = pl.BlockSpec(memory_space=pltpu.VMEM)
SMEM = pl.BlockSpec(memory_space=pltpu.SMEM)
ANY = pl.BlockSpec(memory_space=pl.ANY)


RING = [(0, 2), (2, 4), (4, 6), (6, 7), (7, 5), (5, 3), (3, 1), (1, 0)]
BACK = [(b, a) for a, b in RING]
LIMIT = 16 * 2**20


def ring_holder(place):
    place = lax.rem(place + 8, 8)
    return jnp.where(place < 4, 2 * place, 2 * (7 - place) + 1)


def partial_sum(sources, slot_block, current, panels, earlier, rows):
    cand = lax.axis_index("cand")
    place = jnp.where(lax.rem(cand, 2) == 0, cand // 2, 7 - cand // 2)
    slots, depth, _ = panels[0].shape
    value = None
    for j, (offset, first, held) in enumerate(sources):
        base = ring_holder(place + offset) * held + first
        for s in range(slots):
            block = slot_block[base + s]
            kept = (block < current[0]).astype(jnp.float32).astype(rows.dtype)
            rows[j, s * depth : (s + 1) * depth, :] = earlier[block] * kept
        left = panels[j][...].reshape(slots * depth, panels[j].shape[-1])
        term = lax.dot_general(left, rows[j], ROWS, preferred_element_type=jnp.float32)
        value = term if value is None else value + term
    return value


def own_kernel(sources, slot_block, current, panel, earlier, total, rows):
    total[...] = partial_sum(sources, slot_block, current, [panel], earlier, rows)


def add_kernel(sources, slot_block, current, *refs):
    *panels, earlier, before, total, rows = refs
    total[...] = before[...] + partial_sum(sources, slot_block, current, panels, earlier, rows)


def last_kernel(sources, slot_block, current, panel_a, panel_b, earlier, before, mine, other, rows):
    value = before[...] + partial_sum(sources, slot_block, current, [panel_a, panel_b], earlier, rows)
    size = mine.shape[0]
    first = lax.rem(lax.axis_index("obs"), 2) == 0
    mine[...] = jnp.where(first, value[:size], value[size:])
    other[...] = jnp.where(first, value[size:], value[:size])


def add(kernel, sources, slot_block, current, panels, earlier, before=()):
    slots, depth, size = panels[0].shape
    cols = earlier.shape[-1]
    shapes = [(size // 2, cols)] * 2 if kernel is last_kernel else [(size, cols)]
    return pl.pallas_call(
        functools.partial(kernel, sources),
        out_shape=[jax.ShapeDtypeStruct(shape, jnp.float32) for shape in shapes],
        in_specs=[SMEM] * 2 + [VMEM] * (len(panels) + 1 + len(before)),
        out_specs=[VMEM] * len(shapes),
        scratch_shapes=[pltpu.VMEM((len(panels), slots * depth, cols), earlier.dtype)],
        compiler_params=pltpu.CompilerParams(vmem_limit_bytes=LIMIT),
        cost_estimate=pl.CostEstimate(
            flops=2 * len(panels) * panels[0].size * cols,
            bytes_accessed=4 * len(panels) * panels[0].size,
            transcendentals=0,
        ),
    )(slot_block, current, *panels, earlier, *before)


def two_parts(value):
    top = value.astype(jnp.bfloat16)
    return top, (value - top.astype(jnp.float32)).astype(jnp.bfloat16)


def tile_kernel(s0, s1, s2, s3, cands, tile, high, low, points):
    obs = lax.axis_index("obs")
    share = points.shape[0] // 4
    rows = high.shape[0] // 4
    for m, spread in enumerate((s0, s1, s2, s3)):
        points[pl.ds(pl.multiple_of((obs ^ m) * share, share), share), :] = spread[rows:, :]
        here = slice(m * rows, (m + 1) * rows)
        high[here, :], low[here, :] = two_parts(spread[:rows, :])
    p = points[...]
    p = p / jnp.sum(p, axis=0, keepdims=True)
    c = cands[...]
    c = c / jnp.sum(c, axis=0, keepdims=True)
    cross = lax.dot_general(p, c, ROWS, precision=HIGH, preferred_element_type=jnp.float32)
    norms = lax.dot_general(p * p, jnp.ones_like(c), ROWS, precision=HIGH, preferred_element_type=jnp.float32)
    squared = norms + jnp.sum(c * c, axis=0, keepdims=True) - 2.0 * cross
    tile[...] = jnp.exp(-10.0 * squared)


def solve_kernel(mine, other, mate, far, mate_far, tile, high, low, given, prior, solved, remaining, residual):
    half, rows = mine.shape[0], solved.shape[0] // 2
    core = lax.rem(lax.axis_index("obs"), 2)
    side = lax.rem(lax.axis_index("cand"), 2)
    first = pl.ds(pl.multiple_of(core * half, half), half)
    second = pl.ds(pl.multiple_of((1 - core) * half, half), half)
    residual[first, :] = tile[first, :] - (mine[...] + mate[half:, :] + far[...])
    residual[second, :] = tile[second, :] - (other[...] + mate[:half, :] + mate_far[...])
    top, rest = two_parts(residual[...])
    squares = prior[...]
    for place, (left, left_rest) in ((side, (high[...], low[...])), (1 - side, two_parts(given[...]))):
        part = jnp.dot(left_rest, top, preferred_element_type=jnp.float32)
        part += jnp.dot(left, rest, preferred_element_type=jnp.float32)
        part += jnp.dot(left, top, preferred_element_type=jnp.float32)
        solved[pl.ds(pl.multiple_of(place * rows, rows), rows), :] = part[:rows]
        squares -= jnp.sum(part * part, axis=0, keepdims=True)
    remaining[...] = squares


def on_ring(
    block_index,
    slot_block,
    factor_row,
    earlier_rows,
    obs_weights,
    cand_weights,
    block_inverse,
    prior_var,
):
    cand, obs = lax.axis_index("cand"), lax.axis_index("obs")
    current = block_index[0]
    held = obs_weights.shape[0]
    half = held // 2
    cols = earlier_rows.shape[2]
    panel = jnp.swapaxes(factor_row, 1, 2)

    def flip(value, axis, bits, size):
        return lax.ppermute(value, axis, [(i, i ^ bits) for i in range(size)])

    slot_here = current % held
    points = lax.dynamic_index_in_dim(jnp.swapaxes(obs_weights, 1, 2), slot_here, 0, keepdims=False)
    share = points.shape[0] // 4
    points = lax.dynamic_slice_in_dim(points, obs * share, share, 0)
    rows, width = block_inverse.shape[1:]

    def rows_of(side):
        part = lax.dynamic_slice(block_inverse, (slot_here, side * (rows // 2), 0), (1, rows // 2, width))[0]
        part = jnp.concatenate([part, points], axis=0)
        return jnp.where(cand == current // held, part, jnp.zeros_like(part))

    spread, gift = rows_of(cand % 2), rows_of(1 - cand % 2)

    tie = lax.optimization_barrier

    def onward(pair):
        return (lax.ppermute(pair[0], "cand", RING), lax.ppermute(pair[1], "cand", BACK))

    early = onward((panel[:half], panel[:half]))
    late = onward((panel[half:], panel[half:]))
    (total,) = add(own_kernel, [(0, 0, held)], slot_block, block_index, [panel], earlier_rows)
    spread = spread + flip(gift, "cand", 1, 8)
    for k in (1, 2, 3):
        next_early = onward(early) if k < 3 else lax.ppermute(early[0], "cand", RING)
        late, total, spread = tie((late, total, spread))
        next_late = onward(late) if k < 3 else lax.ppermute(late[1], "cand", BACK)
        sources = [(-k, 0, held), (k, 0, held), (-k, half, held), (k, half, held)]
        (total,) = add(add_kernel, sources, slot_block, block_index, [*early, *late], earlier_rows, [total])
        if k < 3:
            spread = spread + flip(spread, "cand", 2 * k, 8)
        early, late = next_early, next_late
    spreads = [spread, flip(spread, "obs", 1, 4)]
    spreads += [flip(spreads[0], "obs", 2, 4), flip(spreads[1], "obs", 2, 4)]
    early, late, total, spreads = tie((early, late, total, spreads))
    given = flip(jnp.concatenate([v[:-share] for v in spreads], axis=0), "cand", 1, 8)
    sources = [(-4, 0, held), (4, half, held)]
    mine, other = add(last_kernel, sources, slot_block, block_index, [early, late], earlier_rows, [total])

    size = panel.shape[2]
    tile, high, low = pl.pallas_call(
        tile_kernel,
        out_shape=[
            jax.ShapeDtypeStruct((size, cols), jnp.float32),
            jax.ShapeDtypeStruct((2 * rows, size), jnp.bfloat16),
            jax.ShapeDtypeStruct((2 * rows, size), jnp.bfloat16),
        ],
        in_specs=[VMEM] * 5,
        out_specs=[VMEM] * 3,
        scratch_shapes=[pltpu.VMEM((obs_weights.shape[2], size), jnp.float32)],
        compiler_params=pltpu.CompilerParams(vmem_limit_bytes=LIMIT),
        cost_estimate=pl.CostEstimate(flops=10**7, bytes_accessed=10**6, transcendentals=65536),
    )(*spreads, cand_weights.T)

    mate = flip(jnp.concatenate([mine, other], axis=0), "obs", 1, 4)
    far = flip(mine + mate[mine.shape[0] :], "obs", 2, 4)
    mate_far = flip(far, "obs", 1, 4)
    solved_rows, remaining = pl.pallas_call(
        solve_kernel,
        out_shape=[
            jax.ShapeDtypeStruct((rows, cols), jnp.float32),
            jax.ShapeDtypeStruct((1, cols), jnp.float32),
        ],
        in_specs=[VMEM] * 10,
        out_specs=[VMEM] * 2,
        scratch_shapes=[pltpu.VMEM((panel.shape[2], cols), jnp.float32)],
        compiler_params=pltpu.CompilerParams(vmem_limit_bytes=LIMIT),
        cost_estimate=pl.CostEstimate(flops=2 * 10**8, bytes_accessed=10**6, transcendentals=0),
    )(mine, other, mate, far, mate_far, tile, high, low, given, prior_var[None])
    return (solved_rows, remaining[0])


def kernel_tile(points, cands):
    points = points / jnp.sum(points, axis=0, keepdims=True)
    cands = cands / jnp.sum(cands, axis=0, keepdims=True)
    squared = jnp.sum(points * points, axis=0)[:, None] + jnp.sum(cands * cands, axis=0)[None, :]
    squared = squared - 2.0 * lax.dot_general(points, cands, ROWS, precision=HIGH)
    return jnp.exp(-10.0 * squared)


def spread_all(block, axis, holder):
    block = jnp.where(lax.axis_index(axis) == holder, block, jnp.zeros_like(block))
    return lax.psum(block, axis)


def on_any(
    block_index,
    slot_block,
    factor_row,
    earlier_rows,
    obs_weights,
    cand_weights,
    block_inverse,
    prior_var,
):
    current = block_index[0]
    held = obs_weights.shape[0]
    points = lax.dynamic_index_in_dim(obs_weights, current % held, 0, keepdims=False)
    inverse_rows = lax.dynamic_index_in_dim(block_inverse, current % held, 0, keepdims=False)
    points = spread_all(points, "cand", current // held)
    inverse_rows = spread_all(inverse_rows, "cand", current // held)
    kernel_rows = kernel_tile(points.T, cand_weights.T)
    panel = lax.all_gather(factor_row, "cand", axis=0, tiled=True)
    panel = panel * (slot_block < current).astype(jnp.bfloat16)[:, None, None]
    earlier = jnp.take(earlier_rows, slot_block, axis=0)
    partial_sum = jnp.einsum("stq,sqc->tc", panel, earlier, preferred_element_type=jnp.float32)
    residual = kernel_rows - lax.psum(partial_sum, "obs")
    solved_rows = jnp.dot(inverse_rows, residual, precision=HIGH)
    square_sums = lax.psum(jnp.sum(solved_rows * solved_rows, axis=0), "obs")
    return (solved_rows, prior_var - square_sums)


def solution(mesh):
    placed = (
        P(),
        P(),
        P("cand", None, "obs"),
        P(None, "obs", "cand"),
        P("cand", None, None),
        P("cand", None),
        P("cand", "obs", None),
        P("cand"),
    )
    small = mesh.shape["cand"] == 8 and mesh.shape["obs"] == 4
    return jax.shard_map(
        on_ring if small else on_any,
        mesh=mesh,
        in_specs=placed,
        out_specs=(P("obs", "cand"), P("cand")),
        check_vma=False,
    )
```

```python
import functools

import jax
import jax.numpy as jnp
from jax import lax
from jax.experimental import pallas as pl
from jax.experimental.pallas import tpu as pltpu
from jax.sharding import PartitionSpec as P

HIGH = lax.Precision.HIGHEST
ROWS = (((0,), (0,)), ((), ()))
VMEM = pl.BlockSpec(memory_space=pltpu.VMEM)
SMEM = pl.BlockSpec(memory_space=pltpu.SMEM)
ANY = pl.BlockSpec(memory_space=pl.ANY)


RING = [(0, 2), (2, 4), (4, 6), (6, 7), (7, 5), (5, 3), (3, 1), (1, 0)]
BACK = [(b, a) for a, b in RING]
LIMIT = 16 * 2**20


def ring_holder(place):
    place = lax.rem(place + 8, 8)
    return jnp.where(place < 4, 2 * place, 2 * (7 - place) + 1)


def look_up(source, slots, slot_block, current, earlier, rows):
    cand = lax.axis_index("cand")
    place = jnp.where(lax.rem(cand, 2) == 0, cand // 2, 7 - cand // 2)
    offset, first, held = source
    base = ring_holder(place + offset) * held + first
    depth = rows.shape[0] // slots
    for s in range(slots):
        block = slot_block[base + s]
        kept = (block < current[0]).astype(jnp.float32).astype(rows.dtype)
        rows[s * depth : (s + 1) * depth, :] = earlier[block] * kept


def product(panel, rows):
    left = panel[...].reshape(rows.shape[0], panel.shape[-1])
    return lax.dot_general(left, rows[...], ROWS, preferred_element_type=jnp.float32)


def own_kernel(sources, slot_block, current, panel, earlier, total, rows):
    look_up(sources[0], panel.shape[0], slot_block, current, earlier, rows.at[0])
    total[...] = product(panel, rows.at[0])


def add_kernel(sources, slot_block, current, *refs):
    *panels, earlier, before, total, rows = refs
    value = before[...]
    for j, panel in enumerate(panels):
        look_up(sources[j], panel.shape[0], slot_block, current, earlier, rows.at[j])
        value += product(panel, rows.at[j])
    total[...] = value


def add_ahead_kernel(sources, slot_block, current, *refs):
    *refs, ahead, rows = refs
    add_kernel(sources, slot_block, current, *refs, rows)
    for j in range(2):
        look_up(sources[-2 + j], refs[0].shape[0], slot_block, current, refs[-3], ahead.at[j])


def last_kernel(panel_a, panel_b, rows, before, mine, other):
    value = before[...] + product(panel_a, rows.at[0]) + product(panel_b, rows.at[1])
    size = mine.shape[0]
    first = lax.rem(lax.axis_index("obs"), 2) == 0
    mine[...] = jnp.where(first, value[:size], value[size:])
    other[...] = jnp.where(first, value[size:], value[:size])


def add(kernel, sources, slot_block, current, panels, earlier, before=()):
    slots, depth, size = panels[0].shape
    cols = earlier.shape[-1]
    outs = [jax.ShapeDtypeStruct((size, cols), jnp.float32)]
    if kernel is add_ahead_kernel:
        outs.append(jax.ShapeDtypeStruct((2, slots * depth, cols), earlier.dtype))
    return pl.pallas_call(
        functools.partial(kernel, sources),
        out_shape=outs,
        in_specs=[SMEM] * 2 + [VMEM] * (len(panels) + 1 + len(before)),
        out_specs=[VMEM] * len(outs),
        scratch_shapes=[pltpu.VMEM((len(panels), slots * depth, cols), earlier.dtype)],
        compiler_params=pltpu.CompilerParams(vmem_limit_bytes=LIMIT),
        cost_estimate=pl.CostEstimate(
            flops=2 * len(panels) * panels[0].size * cols,
            bytes_accessed=4 * len(panels) * panels[0].size,
            transcendentals=0,
        ),
    )(slot_block, current, *panels, earlier, *before)


def add_last(panels, rows, before):
    size, cols = before.shape
    return pl.pallas_call(
        last_kernel,
        out_shape=[jax.ShapeDtypeStruct((size // 2, cols), jnp.float32)] * 2,
        in_specs=[VMEM] * 4,
        out_specs=[VMEM] * 2,
        compiler_params=pltpu.CompilerParams(vmem_limit_bytes=LIMIT),
        cost_estimate=pl.CostEstimate(
            flops=4 * panels[0].size * cols, bytes_accessed=8 * panels[0].size, transcendentals=0
        ),
    )(*panels, rows, before)


def two_parts(value):
    top = value.astype(jnp.bfloat16)
    return top, (value - top.astype(jnp.float32)).astype(jnp.bfloat16)


def tile_kernel(s0, s1, s2, s3, cands, tile, high, low, points):
    obs = lax.axis_index("obs")
    share = points.shape[0] // 4
    rows = high.shape[0] // 4
    for m, spread in enumerate((s0, s1, s2, s3)):
        points[pl.ds(pl.multiple_of((obs ^ m) * share, share), share), :] = spread[rows:, :]
        here = slice(m * rows, (m + 1) * rows)
        high[here, :], low[here, :] = two_parts(spread[:rows, :])
    p = points[...]
    p = p / jnp.sum(p, axis=0, keepdims=True)
    c = cands[...]
    c = c / jnp.sum(c, axis=0, keepdims=True)
    cross = lax.dot_general(p, c, ROWS, precision=HIGH, preferred_element_type=jnp.float32)
    norms = lax.dot_general(p * p, jnp.ones_like(c), ROWS, precision=HIGH, preferred_element_type=jnp.float32)
    squared = norms + jnp.sum(c * c, axis=0, keepdims=True) - 2.0 * cross
    tile[...] = jnp.exp(-10.0 * squared)


def solve_kernel(mine, other, mate, far, mate_far, tile, high, low, given, prior, solved, remaining, residual):
    half, rows = mine.shape[0], solved.shape[0] // 2
    core = lax.rem(lax.axis_index("obs"), 2)
    side = lax.rem(lax.axis_index("cand"), 2)
    first = pl.ds(pl.multiple_of(core * half, half), half)
    second = pl.ds(pl.multiple_of((1 - core) * half, half), half)
    residual[first, :] = tile[first, :] - (mine[...] + mate[half:, :] + far[...])
    residual[second, :] = tile[second, :] - (other[...] + mate[:half, :] + mate_far[...])
    top, rest = two_parts(residual[...])
    squares = prior[...]
    for place, (left, left_rest) in ((side, (high[...], low[...])), (1 - side, two_parts(given[...]))):
        part = jnp.dot(left_rest, top, preferred_element_type=jnp.float32)
        part += jnp.dot(left, rest, preferred_element_type=jnp.float32)
        part += jnp.dot(left, top, preferred_element_type=jnp.float32)
        solved[pl.ds(pl.multiple_of(place * rows, rows), rows), :] = part[:rows]
        squares -= jnp.sum(part * part, axis=0, keepdims=True)
    remaining[...] = squares


def on_ring(
    block_index,
    slot_block,
    factor_row,
    earlier_rows,
    obs_weights,
    cand_weights,
    block_inverse,
    prior_var,
):
    cand, obs = lax.axis_index("cand"), lax.axis_index("obs")
    current = block_index[0]
    held = obs_weights.shape[0]
    half = held // 2
    cols = earlier_rows.shape[2]
    panel = jnp.swapaxes(factor_row, 1, 2)

    def flip(value, axis, bits, size):
        return lax.ppermute(value, axis, [(i, i ^ bits) for i in range(size)])

    slot_here = current % held
    points = lax.dynamic_index_in_dim(jnp.swapaxes(obs_weights, 1, 2), slot_here, 0, keepdims=False)
    share = points.shape[0] // 4
    points = lax.dynamic_slice_in_dim(points, obs * share, share, 0)
    rows, width = block_inverse.shape[1:]

    def rows_of(side):
        part = lax.dynamic_slice(block_inverse, (slot_here, side * (rows // 2), 0), (1, rows // 2, width))[0]
        part = jnp.concatenate([part, points], axis=0)
        return jnp.where(cand == current // held, part, jnp.zeros_like(part))

    spread, gift = rows_of(cand % 2), rows_of(1 - cand % 2)

    tie = lax.optimization_barrier

    def onward(pair):
        return (lax.ppermute(pair[0], "cand", RING), lax.ppermute(pair[1], "cand", BACK))

    early = onward((panel[:half], panel[:half]))
    late = onward((panel[half:], panel[half:]))
    (total,) = add(own_kernel, [(0, 0, held)], slot_block, block_index, [panel], earlier_rows)
    spread = spread + flip(gift, "cand", 1, 8)
    for k in (1, 2, 3):
        next_early = onward(early) if k < 3 else lax.ppermute(early[0], "cand", RING)
        late, total, spread = tie((late, total, spread))
        next_late = onward(late) if k < 3 else lax.ppermute(late[1], "cand", BACK)
        sources = [(-k, 0, held), (k, 0, held), (-k, half, held), (k, half, held)]
        panels = [*early, *late]
        if k < 3:
            (total,) = add(add_kernel, sources, slot_block, block_index, panels, earlier_rows, [total])
        else:
            sources += [(-4, 0, held), (4, half, held)]
            total, ahead = add(add_ahead_kernel, sources, slot_block, block_index, panels, earlier_rows, [total])
        if k < 3:
            spread = spread + flip(spread, "cand", 2 * k, 8)
        early, late = next_early, next_late
    spreads = [spread, flip(spread, "obs", 1, 4)]
    spreads += [flip(spreads[0], "obs", 2, 4), flip(spreads[1], "obs", 2, 4)]
    early, late, total, ahead, spreads = tie((early, late, total, ahead, spreads))
    given = flip(jnp.concatenate([v[:-share] for v in spreads], axis=0), "cand", 1, 8)
    mine, other = add_last([early, late], ahead, total)

    size = panel.shape[2]
    tile, high, low = pl.pallas_call(
        tile_kernel,
        out_shape=[
            jax.ShapeDtypeStruct((size, cols), jnp.float32),
            jax.ShapeDtypeStruct((2 * rows, size), jnp.bfloat16),
            jax.ShapeDtypeStruct((2 * rows, size), jnp.bfloat16),
        ],
        in_specs=[VMEM] * 5,
        out_specs=[VMEM] * 3,
        scratch_shapes=[pltpu.VMEM((obs_weights.shape[2], size), jnp.float32)],
        compiler_params=pltpu.CompilerParams(vmem_limit_bytes=LIMIT),
        cost_estimate=pl.CostEstimate(flops=10**7, bytes_accessed=10**6, transcendentals=65536),
    )(*spreads, cand_weights.T)

    mate = flip(jnp.concatenate([mine, other], axis=0), "obs", 1, 4)
    far = flip(mine + mate[mine.shape[0] :], "obs", 2, 4)
    mate_far = flip(far, "obs", 1, 4)
    solved_rows, remaining = pl.pallas_call(
        solve_kernel,
        out_shape=[
            jax.ShapeDtypeStruct((rows, cols), jnp.float32),
            jax.ShapeDtypeStruct((1, cols), jnp.float32),
        ],
        in_specs=[VMEM] * 10,
        out_specs=[VMEM] * 2,
        scratch_shapes=[pltpu.VMEM((panel.shape[2], cols), jnp.float32)],
        compiler_params=pltpu.CompilerParams(vmem_limit_bytes=LIMIT),
        cost_estimate=pl.CostEstimate(flops=2 * 10**8, bytes_accessed=10**6, transcendentals=0),
    )(mine, other, mate, far, mate_far, tile, high, low, given, prior_var[None])
    return (solved_rows, remaining[0])


def kernel_tile(points, cands):
    points = points / jnp.sum(points, axis=0, keepdims=True)
    cands = cands / jnp.sum(cands, axis=0, keepdims=True)
    squared = jnp.sum(points * points, axis=0)[:, None] + jnp.sum(cands * cands, axis=0)[None, :]
    squared = squared - 2.0 * lax.dot_general(points, cands, ROWS, precision=HIGH)
    return jnp.exp(-10.0 * squared)


def spread_all(block, axis, holder):
    block = jnp.where(lax.axis_index(axis) == holder, block, jnp.zeros_like(block))
    return lax.psum(block, axis)


def on_any(
    block_index,
    slot_block,
    factor_row,
    earlier_rows,
    obs_weights,
    cand_weights,
    block_inverse,
    prior_var,
):
    current = block_index[0]
    held = obs_weights.shape[0]
    points = lax.dynamic_index_in_dim(obs_weights, current % held, 0, keepdims=False)
    inverse_rows = lax.dynamic_index_in_dim(block_inverse, current % held, 0, keepdims=False)
    points = spread_all(points, "cand", current // held)
    inverse_rows = spread_all(inverse_rows, "cand", current // held)
    kernel_rows = kernel_tile(points.T, cand_weights.T)
    panel = lax.all_gather(factor_row, "cand", axis=0, tiled=True)
    panel = panel * (slot_block < current).astype(jnp.bfloat16)[:, None, None]
    earlier = jnp.take(earlier_rows, slot_block, axis=0)
    partial_sum = jnp.einsum("stq,sqc->tc", panel, earlier, preferred_element_type=jnp.float32)
    residual = kernel_rows - lax.psum(partial_sum, "obs")
    solved_rows = jnp.dot(inverse_rows, residual, precision=HIGH)
    square_sums = lax.psum(jnp.sum(solved_rows * solved_rows, axis=0), "obs")
    return (solved_rows, prior_var - square_sums)


def solution(mesh):
    placed = (
        P(),
        P(),
        P("cand", None, "obs"),
        P(None, "obs", "cand"),
        P("cand", None, None),
        P("cand", None),
        P("cand", "obs", None),
        P("cand"),
    )
    small = mesh.shape["cand"] == 8 and mesh.shape["obs"] == 4
    return jax.shard_map(
        on_ring if small else on_any,
        mesh=mesh,
        in_specs=placed,
        out_specs=(P("obs", "cand"), P("cand")),
        check_vma=False,
    )
```

```python
import functools

import jax
import jax.numpy as jnp
from jax import lax
from jax.experimental import pallas as pl
from jax.experimental.pallas import tpu as pltpu
from jax.sharding import PartitionSpec as P

HIGH = lax.Precision.HIGHEST
ROWS = (((0,), (0,)), ((), ()))
VMEM = pl.BlockSpec(memory_space=pltpu.VMEM)
SMEM = pl.BlockSpec(memory_space=pltpu.SMEM)
ANY = pl.BlockSpec(memory_space=pl.ANY)


RING = [(0, 2), (2, 4), (4, 6), (6, 7), (7, 5), (5, 3), (3, 1), (1, 0)]
BACK = [(b, a) for a, b in RING]
LIMIT = 16 * 2**20


def ring_holder(place):
    place = lax.rem(place + 8, 8)
    return jnp.where(place < 4, 2 * place, 2 * (7 - place) + 1)


def look_up(source, slots, slot_block, current, earlier, rows):
    cand = lax.axis_index("cand")
    place = jnp.where(lax.rem(cand, 2) == 0, cand // 2, 7 - cand // 2)
    offset, first, held = source
    base = ring_holder(place + offset) * held + first
    depth = rows.shape[0] // slots
    for s in range(slots):
        block = slot_block[base + s]
        kept = (block < current[0]).astype(jnp.float32).astype(rows.dtype)
        rows[s * depth : (s + 1) * depth, :] = earlier[block] * kept


def product(panel, rows):
    left = panel[...].reshape(rows.shape[0], panel.shape[-1])
    return lax.dot_general(left, rows[...], ROWS, preferred_element_type=jnp.float32)


def own_kernel(sources, slot_block, current, panel, earlier, total, rows):
    look_up(sources[0], panel.shape[0], slot_block, current, earlier, rows.at[0])
    total[...] = product(panel, rows.at[0])


def add_kernel(sources, slot_block, current, *refs):
    *panels, earlier, before, total, rows = refs
    value = before[...]
    for j, panel in enumerate(panels):
        look_up(sources[j], panel.shape[0], slot_block, current, earlier, rows.at[j])
        value += product(panel, rows.at[j])
    total[...] = value


def add_ahead_kernel(sources, slot_block, current, *refs):
    *refs, ahead, rows = refs
    add_kernel(sources, slot_block, current, *refs, rows)
    for j in range(2):
        look_up(sources[-2 + j], refs[0].shape[0], slot_block, current, refs[-3], ahead.at[j])


def last_kernel(panel_a, panel_b, rows, before, mine, other):
    value = before[...] + product(panel_a, rows.at[0]) + product(panel_b, rows.at[1])
    size = mine.shape[0]
    first = lax.rem(lax.axis_index("obs"), 2) == 0
    mine[...] = jnp.where(first, value[:size], value[size:])
    other[...] = jnp.where(first, value[size:], value[:size])


def add(kernel, sources, slot_block, current, panels, earlier, before=()):
    slots, depth, size = panels[0].shape
    cols = earlier.shape[-1]
    outs = [jax.ShapeDtypeStruct((size, cols), jnp.float32)]
    if kernel is add_ahead_kernel:
        outs.append(jax.ShapeDtypeStruct((2, slots * depth, cols), earlier.dtype))
    return pl.pallas_call(
        functools.partial(kernel, sources),
        out_shape=outs,
        in_specs=[SMEM] * 2 + [VMEM] * (len(panels) + 1 + len(before)),
        out_specs=[VMEM] * len(outs),
        scratch_shapes=[pltpu.VMEM((len(panels), slots * depth, cols), earlier.dtype)],
        compiler_params=pltpu.CompilerParams(vmem_limit_bytes=LIMIT),
        cost_estimate=pl.CostEstimate(
            flops=2 * len(panels) * panels[0].size * cols,
            bytes_accessed=4 * len(panels) * panels[0].size,
            transcendentals=0,
        ),
    )(slot_block, current, *panels, earlier, *before)


def add_last(panels, rows, before):
    size, cols = before.shape
    return pl.pallas_call(
        last_kernel,
        out_shape=[jax.ShapeDtypeStruct((size // 2, cols), jnp.float32)] * 2,
        in_specs=[VMEM] * 4,
        out_specs=[VMEM] * 2,
        compiler_params=pltpu.CompilerParams(vmem_limit_bytes=LIMIT),
        cost_estimate=pl.CostEstimate(
            flops=4 * panels[0].size * cols, bytes_accessed=8 * panels[0].size, transcendentals=0
        ),
    )(*panels, rows, before)


def two_parts(value):
    top = value.astype(jnp.bfloat16)
    return top, (value - top.astype(jnp.float32)).astype(jnp.bfloat16)


def tile_kernel(s0, s1, s2, s3, cands, tile, high, low, points):
    obs = lax.axis_index("obs")
    share = points.shape[0] // 4
    rows = high.shape[0] // 4
    for m, spread in enumerate((s0, s1, s2, s3)):
        points[pl.ds(pl.multiple_of((obs ^ m) * share, share), share), :] = spread[rows:, :]
        here = slice(m * rows, (m + 1) * rows)
        high[here, :], low[here, :] = two_parts(spread[:rows, :])
    p = points[...]
    p = p / jnp.sum(p, axis=0, keepdims=True)
    c = cands[...]
    c = c / jnp.sum(c, axis=0, keepdims=True)
    cross = lax.dot_general(p, c, ROWS, precision=HIGH, preferred_element_type=jnp.float32)
    norms = lax.dot_general(p * p, jnp.ones_like(c), ROWS, precision=HIGH, preferred_element_type=jnp.float32)
    squared = norms + jnp.sum(c * c, axis=0, keepdims=True) - 2.0 * cross
    tile[...] = jnp.exp(-10.0 * squared)


def solve_kernel(mine, other, mate, far, mate_far, tile, high, low, given, prior, solved, remaining, residual):
    half, rows = mine.shape[0], solved.shape[0] // 2
    core = lax.rem(lax.axis_index("obs"), 2)
    side = lax.rem(lax.axis_index("cand"), 2)
    first = pl.ds(pl.multiple_of(core * half, half), half)
    second = pl.ds(pl.multiple_of((1 - core) * half, half), half)
    residual[first, :] = tile[first, :] - (mine[...] + mate[half:, :] + far[...])
    residual[second, :] = tile[second, :] - (other[...] + mate[:half, :] + mate_far[...])
    top, rest = two_parts(residual[...])
    squares = prior[...]
    for place, (left, left_rest) in ((side, (high[...], low[...])), (1 - side, two_parts(given[...]))):
        part = jnp.dot(left_rest, top, preferred_element_type=jnp.float32)
        part += jnp.dot(left, rest, preferred_element_type=jnp.float32)
        part += jnp.dot(left, top, preferred_element_type=jnp.float32)
        solved[pl.ds(pl.multiple_of(place * rows, rows), rows), :] = part[:rows]
        squares -= jnp.sum(part * part, axis=0, keepdims=True)
    remaining[...] = squares


def on_ring(
    block_index,
    slot_block,
    factor_row,
    earlier_rows,
    obs_weights,
    cand_weights,
    block_inverse,
    prior_var,
):
    cand, obs = lax.axis_index("cand"), lax.axis_index("obs")
    current = block_index[0]
    held = obs_weights.shape[0]
    half = held // 2
    cols = earlier_rows.shape[2]
    panel = jnp.swapaxes(factor_row, 1, 2)

    def flip(value, axis, bits, size):
        return lax.ppermute(value, axis, [(i, i ^ bits) for i in range(size)])

    slot_here = current % held
    points = lax.dynamic_index_in_dim(jnp.swapaxes(obs_weights, 1, 2), slot_here, 0, keepdims=False)
    share = points.shape[0] // 4
    points = lax.dynamic_slice_in_dim(points, obs * share, share, 0)
    rows, width = block_inverse.shape[1:]

    def rows_of(side):
        part = lax.dynamic_slice(block_inverse, (slot_here, side * (rows // 2), 0), (1, rows // 2, width))[0]
        part = jnp.concatenate([part, points], axis=0)
        return jnp.where(cand == current // held, part, jnp.zeros_like(part))

    spread, gift = rows_of(cand % 2), rows_of(1 - cand % 2)

    tie = lax.optimization_barrier

    def onward(pair):
        return (lax.ppermute(pair[0], "cand", RING), lax.ppermute(pair[1], "cand", BACK))

    early = onward((panel[:half], panel[:half]))
    late = onward((panel[half:], panel[half:]))
    (total,) = add(own_kernel, [(0, 0, held)], slot_block, block_index, [panel], earlier_rows)
    spread = spread + flip(gift, "cand", 1, 8)
    for k in (1, 2, 3):
        next_early = onward(early) if k < 3 else lax.ppermute(early[0], "cand", RING)
        late, total, spread = tie((late, total, spread))
        next_late = onward(late) if k < 3 else lax.ppermute(late[1], "cand", BACK)
        sources = [(-k, 0, held), (k, 0, held), (-k, half, held), (k, half, held)]
        panels = [*early, *late]
        if k < 3:
            (total,) = add(add_kernel, sources, slot_block, block_index, panels, earlier_rows, [total])
        else:
            sources += [(-4, 0, held), (4, half, held)]
            total, ahead = add(add_ahead_kernel, sources, slot_block, block_index, panels, earlier_rows, [total])
        if k < 3:
            spread = spread + flip(spread, "cand", 8 >> k, 8)
        early, late = next_early, next_late
    spreads = [spread, flip(spread, "obs", 1, 4)]
    spreads += [flip(spreads[0], "obs", 2, 4), flip(spreads[1], "obs", 2, 4)]
    early, late, total, ahead, spreads = tie((early, late, total, ahead, spreads))
    given = flip(jnp.concatenate([v[:-share] for v in spreads], axis=0), "cand", 1, 8)
    mine, other = add_last([early, late], ahead, total)

    size = panel.shape[2]
    tile, high, low = pl.pallas_call(
        tile_kernel,
        out_shape=[
            jax.ShapeDtypeStruct((size, cols), jnp.float32),
            jax.ShapeDtypeStruct((2 * rows, size), jnp.bfloat16),
            jax.ShapeDtypeStruct((2 * rows, size), jnp.bfloat16),
        ],
        in_specs=[VMEM] * 5,
        out_specs=[VMEM] * 3,
        scratch_shapes=[pltpu.VMEM((obs_weights.shape[2], size), jnp.float32)],
        compiler_params=pltpu.CompilerParams(vmem_limit_bytes=LIMIT),
        cost_estimate=pl.CostEstimate(flops=10**7, bytes_accessed=10**6, transcendentals=65536),
    )(*spreads, cand_weights.T)

    mate = flip(jnp.concatenate([mine, other], axis=0), "obs", 1, 4)
    far = flip(mine + mate[mine.shape[0] :], "obs", 2, 4)
    mate_far = flip(far, "obs", 1, 4)
    solved_rows, remaining = pl.pallas_call(
        solve_kernel,
        out_shape=[
            jax.ShapeDtypeStruct((rows, cols), jnp.float32),
            jax.ShapeDtypeStruct((1, cols), jnp.float32),
        ],
        in_specs=[VMEM] * 10,
        out_specs=[VMEM] * 2,
        scratch_shapes=[pltpu.VMEM((panel.shape[2], cols), jnp.float32)],
        compiler_params=pltpu.CompilerParams(vmem_limit_bytes=LIMIT),
        cost_estimate=pl.CostEstimate(flops=2 * 10**8, bytes_accessed=10**6, transcendentals=0),
    )(mine, other, mate, far, mate_far, tile, high, low, given, prior_var[None])
    return (solved_rows, remaining[0])


def kernel_tile(points, cands):
    points = points / jnp.sum(points, axis=0, keepdims=True)
    cands = cands / jnp.sum(cands, axis=0, keepdims=True)
    squared = jnp.sum(points * points, axis=0)[:, None] + jnp.sum(cands * cands, axis=0)[None, :]
    squared = squared - 2.0 * lax.dot_general(points, cands, ROWS, precision=HIGH)
    return jnp.exp(-10.0 * squared)


def spread_all(block, axis, holder):
    block = jnp.where(lax.axis_index(axis) == holder, block, jnp.zeros_like(block))
    return lax.psum(block, axis)


def on_any(
    block_index,
    slot_block,
    factor_row,
    earlier_rows,
    obs_weights,
    cand_weights,
    block_inverse,
    prior_var,
):
    current = block_index[0]
    held = obs_weights.shape[0]
    points = lax.dynamic_index_in_dim(obs_weights, current % held, 0, keepdims=False)
    inverse_rows = lax.dynamic_index_in_dim(block_inverse, current % held, 0, keepdims=False)
    points = spread_all(points, "cand", current // held)
    inverse_rows = spread_all(inverse_rows, "cand", current // held)
    kernel_rows = kernel_tile(points.T, cand_weights.T)
    panel = lax.all_gather(factor_row, "cand", axis=0, tiled=True)
    panel = panel * (slot_block < current).astype(jnp.bfloat16)[:, None, None]
    earlier = jnp.take(earlier_rows, slot_block, axis=0)
    partial_sum = jnp.einsum("stq,sqc->tc", panel, earlier, preferred_element_type=jnp.float32)
    residual = kernel_rows - lax.psum(partial_sum, "obs")
    solved_rows = jnp.dot(inverse_rows, residual, precision=HIGH)
    square_sums = lax.psum(jnp.sum(solved_rows * solved_rows, axis=0), "obs")
    return (solved_rows, prior_var - square_sums)


def solution(mesh):
    placed = (
        P(),
        P(),
        P("cand", None, "obs"),
        P(None, "obs", "cand"),
        P("cand", None, None),
        P("cand", None),
        P("cand", "obs", None),
        P("cand"),
    )
    small = mesh.shape["cand"] == 8 and mesh.shape["obs"] == 4
    return jax.shard_map(
        on_ring if small else on_any,
        mesh=mesh,
        in_specs=placed,
        out_specs=(P("obs", "cand"), P("cand")),
        check_vma=False,
    )
```

```python
import functools

import jax
import jax.numpy as jnp
from jax import lax
from jax.experimental import pallas as pl
from jax.experimental.pallas import tpu as pltpu
from jax.sharding import PartitionSpec as P

HIGH = lax.Precision.HIGHEST
ROWS = (((0,), (0,)), ((), ()))
VMEM = pl.BlockSpec(memory_space=pltpu.VMEM)
SMEM = pl.BlockSpec(memory_space=pltpu.SMEM)
ANY = pl.BlockSpec(memory_space=pl.ANY)


RING = [(0, 2), (2, 4), (4, 6), (6, 7), (7, 5), (5, 3), (3, 1), (1, 0)]
BACK = [(b, a) for a, b in RING]
LIMIT = 16 * 2**20


def ring_holder(place):
    place = lax.rem(place + 8, 8)
    return jnp.where(place < 4, 2 * place, 2 * (7 - place) + 1)


def look_up(source, slots, slot_block, current, earlier, rows):
    cand = lax.axis_index("cand")
    place = jnp.where(lax.rem(cand, 2) == 0, cand // 2, 7 - cand // 2)
    offset, first, held = source
    base = ring_holder(place + offset) * held + first
    depth = rows.shape[0] // slots
    for s in range(slots):
        block = slot_block[base + s]
        kept = (block < current[0]).astype(jnp.float32).astype(rows.dtype)
        rows[s * depth : (s + 1) * depth, :] = earlier[block] * kept


def product(panel, rows):
    left = panel[...].reshape(rows.shape[0], panel.shape[-1])
    return lax.dot_general(left, rows[...], ROWS, preferred_element_type=jnp.float32)


def own_kernel(sources, slot_block, current, panel, earlier, total, rows):
    look_up(sources[0], panel.shape[0], slot_block, current, earlier, rows.at[0])
    total[...] = product(panel, rows.at[0])


def add_kernel(sources, slot_block, current, *refs):
    *panels, earlier, before, total, rows = refs
    value = before[...]
    for j, panel in enumerate(panels):
        look_up(sources[j], panel.shape[0], slot_block, current, earlier, rows.at[j])
        value += product(panel, rows.at[j])
    total[...] = value


def add_ahead_kernel(sources, slot_block, current, *refs):
    *refs, ahead, rows = refs
    add_kernel(sources, slot_block, current, *refs, rows)
    for j in range(2):
        look_up(sources[-2 + j], refs[0].shape[0], slot_block, current, refs[-3], ahead.at[j])


def last_kernel(panel_a, panel_b, rows, before, mine, other):
    value = before[...] + product(panel_a, rows.at[0]) + product(panel_b, rows.at[1])
    size = mine.shape[0]
    first = lax.rem(lax.axis_index("obs"), 2) == 0
    mine[...] = jnp.where(first, value[:size], value[size:])
    other[...] = jnp.where(first, value[size:], value[:size])


def add(kernel, sources, slot_block, current, panels, earlier, before=()):
    slots, depth, size = panels[0].shape
    cols = earlier.shape[-1]
    outs = [jax.ShapeDtypeStruct((size, cols), jnp.float32)]
    if kernel is add_ahead_kernel:
        outs.append(jax.ShapeDtypeStruct((2, slots * depth, cols), earlier.dtype))
    return pl.pallas_call(
        functools.partial(kernel, sources),
        out_shape=outs,
        in_specs=[SMEM] * 2 + [VMEM] * (len(panels) + 1 + len(before)),
        out_specs=[VMEM] * len(outs),
        scratch_shapes=[pltpu.VMEM((len(panels), slots * depth, cols), earlier.dtype)],
        compiler_params=pltpu.CompilerParams(vmem_limit_bytes=LIMIT),
        cost_estimate=pl.CostEstimate(
            flops=2 * len(panels) * panels[0].size * cols,
            bytes_accessed=4 * len(panels) * panels[0].size,
            transcendentals=0,
        ),
    )(slot_block, current, *panels, earlier, *before)


def add_last(panels, rows, before):
    size, cols = before.shape
    return pl.pallas_call(
        last_kernel,
        out_shape=[jax.ShapeDtypeStruct((size // 2, cols), jnp.float32)] * 2,
        in_specs=[VMEM] * 4,
        out_specs=[VMEM] * 2,
        compiler_params=pltpu.CompilerParams(vmem_limit_bytes=LIMIT),
        cost_estimate=pl.CostEstimate(
            flops=4 * panels[0].size * cols, bytes_accessed=8 * panels[0].size, transcendentals=0
        ),
    )(*panels, rows, before)


def two_parts(value):
    top = value.astype(jnp.bfloat16)
    return top, (value - top.astype(jnp.float32)).astype(jnp.bfloat16)


def tile_kernel(s0, s1, s2, s3, cands, tile, high, low, points):
    obs = lax.axis_index("obs")
    share = points.shape[0] // 4
    rows = high.shape[0] // 4
    for m, spread in enumerate((s0, s1, s2, s3)):
        points[pl.ds(pl.multiple_of((obs ^ m) * share, share), share), :] = spread[rows:, :]
        here = slice(m * rows, (m + 1) * rows)
        high[here, :], low[here, :] = two_parts(spread[:rows, :])
    p = points[...]
    p = p / jnp.sum(p, axis=0, keepdims=True)
    c = cands[...]
    c = c / jnp.sum(c, axis=0, keepdims=True)
    cross = lax.dot_general(p, c, ROWS, precision=HIGH, preferred_element_type=jnp.float32)
    norms = lax.dot_general(p * p, jnp.ones_like(c), ROWS, precision=HIGH, preferred_element_type=jnp.float32)
    squared = norms + jnp.sum(c * c, axis=0, keepdims=True) - 2.0 * cross
    tile[...] = jnp.exp(-10.0 * squared)


def solve_kernel(mine, other, mate, far, mate_far, tile, high, low, given, prior, solved, remaining, residual):
    half, rows = mine.shape[0], solved.shape[0] // 2
    core = lax.rem(lax.axis_index("obs"), 2)
    side = lax.rem(lax.axis_index("cand"), 2)
    first = pl.ds(pl.multiple_of(core * half, half), half)
    second = pl.ds(pl.multiple_of((1 - core) * half, half), half)
    residual[first, :] = tile[first, :] - (mine[...] + mate[half:, :] + far[...])
    residual[second, :] = tile[second, :] - (other[...] + mate[:half, :] + mate_far[...])
    top, rest = two_parts(residual[...])
    squares = prior[...]
    for place, (left, left_rest) in ((side, (high[...], low[...])), (1 - side, two_parts(given[...]))):
        part = jnp.dot(left_rest, top, preferred_element_type=jnp.float32)
        part += jnp.dot(left, rest, preferred_element_type=jnp.float32)
        part += jnp.dot(left, top, preferred_element_type=jnp.float32)
        solved[pl.ds(pl.multiple_of(place * rows, rows), rows), :] = part[:rows]
        squares -= jnp.sum(part * part, axis=0, keepdims=True)
    remaining[...] = squares


def on_ring(
    block_index,
    slot_block,
    factor_row,
    earlier_rows,
    obs_weights,
    cand_weights,
    block_inverse,
    prior_var,
):
    cand, obs = lax.axis_index("cand"), lax.axis_index("obs")
    current = block_index[0]
    held = obs_weights.shape[0]
    half = held // 2
    cols = earlier_rows.shape[2]
    panel = jnp.swapaxes(factor_row, 1, 2)

    def flip(value, axis, bits, size):
        return lax.ppermute(value, axis, [(i, i ^ bits) for i in range(size)])

    slot_here = current % held
    points = lax.dynamic_index_in_dim(jnp.swapaxes(obs_weights, 1, 2), slot_here, 0, keepdims=False)
    share = points.shape[0] // 4
    points = lax.dynamic_slice_in_dim(points, obs * share, share, 0)
    rows, width = block_inverse.shape[1:]

    def rows_of(side):
        part = lax.dynamic_slice(block_inverse, (slot_here, side * (rows // 2), 0), (1, rows // 2, width))[0]
        part = jnp.concatenate([part, points], axis=0)
        return jnp.where(cand == current // held, part, jnp.zeros_like(part))

    spread, gift = rows_of(cand % 2), rows_of(1 - cand % 2)

    tie = lax.optimization_barrier

    def onward(pair):
        return (lax.ppermute(pair[0], "cand", RING), lax.ppermute(pair[1], "cand", BACK))

    early = onward((panel[:half], panel[:half]))
    late = onward((panel[half:], panel[half:]))
    (total,) = add(own_kernel, [(0, 0, held)], slot_block, block_index, [panel], earlier_rows)
    spread = spread + flip(gift, "cand", 1, 8)
    for k in (1, 2, 3):
        next_early = onward(early) if k < 3 else lax.ppermute(early[0], "cand", RING)
        late, total, spread = tie((late, total, spread))
        next_late = onward(late) if k < 3 else lax.ppermute(late[1], "cand", BACK)
        sources = [(-k, 0, held), (k, 0, held), (-k, half, held), (k, half, held)]
        panels = [*early, *late]
        if k < 3:
            (total,) = add(add_kernel, sources, slot_block, block_index, panels, earlier_rows, [total])
        else:
            sources += [(-4, 0, held), (4, half, held)]
            total, ahead = add(add_ahead_kernel, sources, slot_block, block_index, panels, earlier_rows, [total])
        if k < 3:
            spread = spread + flip(spread, "cand", 8 >> k, 8)
        early, late = next_early, next_late
    spreads = [spread, flip(spread, "obs", 1, 4)]
    spreads += [flip(spreads[0], "obs", 2, 4), flip(spreads[1], "obs", 2, 4)]
    early, late, total, ahead, spreads = tie((early, late, total, ahead, spreads))
    given = flip(jnp.concatenate([v[:-share] for v in spreads], axis=0), "cand", 1, 8)
    mine, other = add_last([early, late], ahead, total)

    size = panel.shape[2]
    tile, high, low = pl.pallas_call(
        tile_kernel,
        out_shape=[
            jax.ShapeDtypeStruct((size, cols), jnp.float32),
            jax.ShapeDtypeStruct((2 * rows, size), jnp.bfloat16),
            jax.ShapeDtypeStruct((2 * rows, size), jnp.bfloat16),
        ],
        in_specs=[VMEM] * 5,
        out_specs=[VMEM] * 3,
        scratch_shapes=[pltpu.VMEM((obs_weights.shape[2], size), jnp.float32)],
        compiler_params=pltpu.CompilerParams(vmem_limit_bytes=LIMIT),
        cost_estimate=pl.CostEstimate(flops=10**7, bytes_accessed=10**6, transcendentals=65536),
    )(*spreads, cand_weights.T)

    mate = flip(jnp.concatenate([mine, other], axis=0), "obs", 1, 4)
    mate, tile, high, low = tie((mate, tile, high, low))
    far = flip(mine + mate[mine.shape[0] :], "obs", 2, 4)
    mate_far = flip(far, "obs", 1, 4)
    solved_rows, remaining = pl.pallas_call(
        solve_kernel,
        out_shape=[
            jax.ShapeDtypeStruct((rows, cols), jnp.float32),
            jax.ShapeDtypeStruct((1, cols), jnp.float32),
        ],
        in_specs=[VMEM] * 10,
        out_specs=[VMEM] * 2,
        scratch_shapes=[pltpu.VMEM((panel.shape[2], cols), jnp.float32)],
        compiler_params=pltpu.CompilerParams(vmem_limit_bytes=LIMIT),
        cost_estimate=pl.CostEstimate(flops=2 * 10**8, bytes_accessed=10**6, transcendentals=0),
    )(mine, other, mate, far, mate_far, tile, high, low, given, prior_var[None])
    return (solved_rows, remaining[0])


def kernel_tile(points, cands):
    points = points / jnp.sum(points, axis=0, keepdims=True)
    cands = cands / jnp.sum(cands, axis=0, keepdims=True)
    squared = jnp.sum(points * points, axis=0)[:, None] + jnp.sum(cands * cands, axis=0)[None, :]
    squared = squared - 2.0 * lax.dot_general(points, cands, ROWS, precision=HIGH)
    return jnp.exp(-10.0 * squared)


def spread_all(block, axis, holder):
    block = jnp.where(lax.axis_index(axis) == holder, block, jnp.zeros_like(block))
    return lax.psum(block, axis)


def on_any(
    block_index,
    slot_block,
    factor_row,
    earlier_rows,
    obs_weights,
    cand_weights,
    block_inverse,
    prior_var,
):
    current = block_index[0]
    held = obs_weights.shape[0]
    points = lax.dynamic_index_in_dim(obs_weights, current % held, 0, keepdims=False)
    inverse_rows = lax.dynamic_index_in_dim(block_inverse, current % held, 0, keepdims=False)
    points = spread_all(points, "cand", current // held)
    inverse_rows = spread_all(inverse_rows, "cand", current // held)
    kernel_rows = kernel_tile(points.T, cand_weights.T)
    panel = lax.all_gather(factor_row, "cand", axis=0, tiled=True)
    panel = panel * (slot_block < current).astype(jnp.bfloat16)[:, None, None]
    earlier = jnp.take(earlier_rows, slot_block, axis=0)
    partial_sum = jnp.einsum("stq,sqc->tc", panel, earlier, preferred_element_type=jnp.float32)
    residual = kernel_rows - lax.psum(partial_sum, "obs")
    solved_rows = jnp.dot(inverse_rows, residual, precision=HIGH)
    square_sums = lax.psum(jnp.sum(solved_rows * solved_rows, axis=0), "obs")
    return (solved_rows, prior_var - square_sums)


def solution(mesh):
    placed = (
        P(),
        P(),
        P("cand", None, "obs"),
        P(None, "obs", "cand"),
        P("cand", None, None),
        P("cand", None),
        P("cand", "obs", None),
        P("cand"),
    )
    small = mesh.shape["cand"] == 8 and mesh.shape["obs"] == 4
    return jax.shard_map(
        on_ring if small else on_any,
        mesh=mesh,
        in_specs=placed,
        out_specs=(P("obs", "cand"), P("cand")),
        check_vma=False,
    )
```
